32 devices in a mesh: narrow: 8 (over z, y), wide: 4 (over x, core).
Axes of the slice: x: 2, y: 2, z: 4, core: 2. Of those that a mesh axis runs over, the one named last changes fastest.
Arguments:
- tokens: bfloat16 [8192, 1024], P('narrow'), may hold values from -6 to 6
- page_len: int32 [16], P('narrow'), may hold values from 1 to 512, as said below
- w_qkv: bfloat16 [3, 1024, 1024], P(None, None, 'wide'), may hold values from -0.1875 to 0.1875
- b_qv: float32 [2, 1024], P(None, 'wide'), may hold values from -3 to 3
- w_out: bfloat16 [1024, 1024], P('wide'), may hold values from -0.5 to 0.5
- b_out: float32 [1024], replicated, may hold values from -3 to 3
- gain_attn: float32 [1024], replicated, may hold values from 0.25 to 1.75
- shift_attn: float32 [1024], replicated, may hold values from -2 to 2
- w_up: bfloat16 [1024, 4096], P(None, 'wide'), may hold values from -0.1875 to 0.1875
- b_up: float32 [4096], P('wide'), may hold values from -3 to 3
- w_down: bfloat16 [4096, 1024], P('wide'), may hold values from -0.09375 to 0.09375
- b_down: float32 [1024], replicated, may hold values from -3 to 3
- gain_ffn: float32 [1024], replicated, may hold values from 0.25 to 1.75
- shift_ffn: float32 [1024], replicated, may hold values from -2 to 2
- cotangent: bfloat16 [8192, 1024], P('narrow'), may hold values from -6 to 6
Outputs:
- layer_out: bfloat16 [8192, 1024], P('narrow')
- grad_tokens: bfloat16 [8192, 1024], P('narrow')
- grad_qkv_w: float32 [3, 1024, 1024], P(None, None, 'wide')
- grad_qv_bias: float32 [2, 1024], P(None, 'wide')
- grad_out_w: float32 [1024, 1024], P('wide')
- grad_out_bias: float32 [1024], replicated
- grad_gain_attn: float32 [1024], replicated
- grad_shift_attn: float32 [1024], replicated
- grad_up_w: float32 [1024, 4096], P(None, 'wide')
- grad_up_bias: float32 [4096], P('wide')
- grad_down_w: float32 [4096, 1024], P('wide')
- grad_down_bias: float32 [1024], replicated
- grad_gain_ffn: float32 [1024], replicated
- grad_shift_ffn: float32 [1024], replicated
The draws below stay inside these ranges and needn't reach their ends.
Inputs may be any that keep to these rules, and one draw needn't show every extreme that they name: `page_len`: each page holds 1 to 512 valid tokens at its start, most pages far fewer; in every draw some page is full.
All inputs are finite; a program needn't handle non-finite values.
Results may differ from the reference program's by a relative error of at most 0.012.
The reference program's roundings to bfloat16 on the way count: a program that leaves them out, or rounds other values in their place, can miss the bound.
Values may be sent and summed in bfloat16 or wider, within the bound.
No kernel may reach another device: no remote copies, remote signals or barrier semaphores. Data moves between devices by JAX's collectives and lax.ppermute only.
A program may use at most 128 MiB of HBM per device.

```python
import jax
import jax.numpy as jnp
from jax import lax

D = 1024
HEADS = 16
HEAD_DIM = 64
FF = 4096
PAGE_LEN = 512
PAGES_DEV = 2
PAGES = 16
TOKENS = 8192
N_NARROW = 8


def draw_page_len(key, part):
    shift_key, cut_key, full_key = jax.random.split(key, 3)
    shifts = jax.random.randint(shift_key, (PAGES,), 0, 6)
    ceilings = jnp.maximum(jnp.right_shift(jnp.full((PAGES,), PAGE_LEN, jnp.int32), shifts.astype(jnp.int32)), 1)
    cuts = jax.random.randint(cut_key, (PAGES,), 0, ceilings // 2 + 1)
    lengths = jnp.maximum(ceilings - cuts, 1)
    full_page = jax.random.randint(full_key, (), 0, PAGES)
    return jnp.where(jnp.arange(PAGES, dtype=jnp.int32) == full_page, PAGE_LEN, lengths).astype(jnp.int32)


def steps_of(stream_key, dims, cuts, smallest, high):
    factor_of, own = 1.0, jax.random.fold_in(stream_key, 6)
    for position, blocks in cuts:
        heights = jnp.exp(jax.random.uniform(jax.random.fold_in(own, position), (blocks,), jnp.float32, smallest / len(cuts), high / len(cuts)))
        factor_of = factor_of * jnp.repeat(heights, dims[position] // blocks).reshape([-1 if axis == position else 1 for axis in range(len(dims))])
    return factor_of


def gaussian(rng, dims, deviation, reach, cuts=(), held_as=jnp.bfloat16):
    values = deviation * jax.random.normal(rng, dims, jnp.float32)
    if cuts:
        values = values * steps_of(rng, dims, cuts, -0.22, 0.18)
    return jnp.clip(values, -reach, reach).astype(held_as)


def setup_inputs(seed: int = 0) -> dict:
    key_of = jax.random.split(jax.random.key(seed), 16)
    return {
        "tokens": gaussian(key_of[0], (TOKENS, D), 1.0, 6.0, ((0, 8),)),
        "page_len": draw_page_len(jax.random.fold_in(key_of[15], 71), 0),
        "w_qkv": gaussian(key_of[2], (3, D, HEADS * HEAD_DIM), D ** -0.5, 0.1875, ((2, 4),)),
        "b_qv": gaussian(key_of[3], (2, HEADS * HEAD_DIM), 0.5, 3.0, ((1, 4),), jnp.float32),
        "w_out": gaussian(key_of[4], (HEADS * HEAD_DIM, D), (HEADS * HEAD_DIM // 8) ** -0.5, 0.5, ((0, 4),)),
        "b_out": gaussian(key_of[5], (D,), 0.5, 3.0, (), jnp.float32),
        "gain_attn": jnp.clip(1.0 + 0.15 * jax.random.normal(key_of[6], (D,), jnp.float32), 0.25, 1.75),
        "shift_attn": gaussian(key_of[7], (D,), 0.3, 2.0, (), jnp.float32),
        "w_up": gaussian(key_of[8], (D, FF), D ** -0.5, 0.1875, ((1, 4),)),
        "b_up": gaussian(key_of[9], (FF,), 0.5, 3.0, ((0, 4),), jnp.float32),
        "w_down": gaussian(key_of[10], (FF, D), FF ** -0.5, 0.09375, ((0, 4),)),
        "b_down": gaussian(key_of[11], (D,), 0.5, 3.0, (), jnp.float32),
        "gain_ffn": jnp.clip(1.0 + 0.15 * jax.random.normal(key_of[12], (D,), jnp.float32), 0.25, 1.75),
        "shift_ffn": gaussian(key_of[13], (D,), 0.3, 2.0, (), jnp.float32),
        "cotangent": gaussian(key_of[14], (TOKENS, D), 1.0, 6.0, ((0, 8),)),
    }


HIGH = lax.Precision.HIGHEST

@jax.custom_vjp
def low(v):
    return lax.optimization_barrier(v.astype(jnp.bfloat16)).astype(jnp.float32)

@jax.custom_vjp
def low_back(v):
    return v

def low_keep(v):
    return (low(v), None)

def low_pass(kept, grad):
    return (grad,)

def back_keep(v):
    return (v, None)

def back_low(kept, grad):
    return (low(grad),)
low.defvjp(low_keep, low_pass)
low_back.defvjp(back_keep, back_low)

def norm_rows(summed, gain_row, shift_row):
    row_mean = lax.optimization_barrier(jnp.mean(summed, axis=-1, keepdims=True))
    centered = summed - row_mean
    variance = lax.optimization_barrier(jnp.mean(centered * centered, axis=-1, keepdims=True))
    return centered * lax.rsqrt(variance + 1e-12) * gain_row + shift_row

def page_attention(page_item):
    page_block, page_length = page_item
    query_rows, key_rows, value_rows = (page_block[0], page_block[1], page_block[2])
    raw_scores = low_back(jnp.einsum('qhe,khe->hqk', query_rows, key_rows, precision=HIGH) * HEAD_DIM ** (-0.5))
    key_valid = jnp.arange(key_rows.shape[0], dtype=jnp.int32) < page_length
    masked = jnp.where(key_valid[None, None, :], raw_scores, -1e+30)
    row_max = lax.optimization_barrier(jnp.max(masked, axis=-1, keepdims=True))
    exponent = jnp.exp(masked - row_max)
    attend = low(exponent / lax.optimization_barrier(jnp.sum(exponent, axis=-1, keepdims=True)))
    mixed_heads = jnp.einsum('hqk,khe->qhe', attend, value_rows, precision=HIGH)
    return mixed_heads.reshape(mixed_heads.shape[0], HEADS * HEAD_DIM)

def forward(token_rows, page_lengths, params):
    w_qkv, b_qv, w_out, b_out, gain_attn, shift_attn, w_up, b_up, w_down, b_down, gain_ffn, shift_ffn = params
    page_count = page_lengths.shape[0]
    paged_tokens = token_rows.reshape(page_count, PAGE_LEN, D)
    biases = jnp.stack([b_qv[0], jnp.zeros_like(b_qv[0]), b_qv[1]])
    projected = jnp.einsum('pld,cdh->pclh', paged_tokens, w_qkv, precision=HIGH) + biases[None, :, None, :]
    qkv_heads = low(low_back(projected)).reshape(page_count, 3, PAGE_LEN, HEADS, HEAD_DIM)
    mixed_heads = lax.map(jax.checkpoint(page_attention), (qkv_heads, page_lengths))
    mixed_heads = low(low_back(mixed_heads.reshape(page_count * PAGE_LEN, HEADS * HEAD_DIM)))
    attn_sum = low_back(jnp.dot(mixed_heads, w_out, precision=HIGH))
    hidden = norm_rows(attn_sum + b_out + token_rows, gain_attn, shift_attn)
    pre_active = low_back(jnp.dot(low(hidden), w_up, precision=HIGH) + b_up)
    active = low(jax.nn.gelu(pre_active, approximate=False))
    down_sum = low_back(jnp.dot(active, w_down, precision=HIGH))
    return norm_rows(down_sum + b_down + hidden, gain_ffn, shift_ffn)

def reference(tokens, page_len, w_qkv, b_qv, w_out, b_out, gain_attn, shift_attn, w_up, b_up, w_down, b_down, gain_ffn, shift_ffn, cotangent):
    params = (w_qkv.astype(jnp.float32), b_qv.astype(jnp.float32), w_out.astype(jnp.float32), b_out.astype(jnp.float32), gain_attn.astype(jnp.float32), shift_attn.astype(jnp.float32), w_up.astype(jnp.float32), b_up.astype(jnp.float32), w_down.astype(jnp.float32), b_down.astype(jnp.float32), gain_ffn.astype(jnp.float32), shift_ffn.astype(jnp.float32))
    group_tokens = tokens.astype(jnp.float32).reshape(N_NARROW, PAGES_DEV * PAGE_LEN, D)
    group_cots = cotangent.astype(jnp.float32).reshape(N_NARROW, PAGES_DEV * PAGE_LEN, D)
    group_lengths = page_len.astype(jnp.int32).reshape(N_NARROW, PAGES_DEV)

    def page_group(grad_total, group_item):
        token_rows, cot_rows, page_lengths = group_item
        layer_rows, pull_back = jax.vjp(lambda rows, weights: forward(rows, page_lengths, weights), token_rows, params)
        grad_rows, grad_params = pull_back(cot_rows)
        grad_total = jax.tree.map(jnp.add, grad_total, grad_params)
        return (grad_total, (layer_rows.astype(jnp.bfloat16), grad_rows.astype(jnp.bfloat16)))
    grad_zero = jax.tree.map(jnp.zeros_like, params)
    grads, (layer_out, grad_tokens) = lax.scan(page_group, grad_zero, (group_tokens, group_cots, group_lengths))
    return (layer_out.reshape(TOKENS, D), grad_tokens.reshape(TOKENS, D), grads[0], grads[1], grads[2], grads[3], grads[4], grads[5], grads[6], grads[7], grads[8], grads[9], grads[10], grads[11])
```

```python
import jax
import jax.numpy as jnp
from jax import lax
from jax.sharding import PartitionSpec as P

HEAD_DIM = 64
CHUNKS = 2

F32 = jnp.float32
B16 = jnp.bfloat16


def dot(a, b, dims):
    return lax.dot_general(a, b, (dims, ((), ())), preferred_element_type=F32)


def mm(a, b):
    return dot(a, b, ((1,), (0,)))


def mm_nt(a, b):
    return dot(a, b, ((1,), (1,)))


def mm_tn(a, b):
    return dot(a, b, ((0,), (0,)))


def swap_bit(value, axis, mask):
    size = lax.axis_size(axis)
    return lax.ppermute(value, axis, [(i, i ^ mask) for i in range(size)])


def masks_of(size):
    return [1 << k for k in range(size.bit_length() - 1)]


def outer_sum(part):
    total = part
    for mask in masks_of(lax.axis_size("wide"))[1:]:
        low = total.astype(B16)
        total = low.astype(F32) + swap_bit(low, "wide", mask).astype(F32)
    return total


def narrow_sum(value):
    masks = masks_of(lax.axis_size("narrow"))
    index = lax.axis_index("narrow")
    bits = [(index // mask) % 2 for mask in masks]
    for mask, bit in zip(masks, bits):
        half = value.shape[0] // 2
        send = lax.dynamic_slice_in_dim(value, (1 - bit) * half, half, 0)
        keep = lax.dynamic_slice_in_dim(value, bit * half, half, 0)
        came = swap_bit(send, "narrow", mask)
        value = (keep.astype(F32) + came.astype(F32)).astype(B16)
    for mask, bit in reversed(list(zip(masks, bits))):
        came = swap_bit(value, "narrow", mask)
        first = jnp.where(bit == 0, value, came)
        second = jnp.where(bit == 0, came, value)
        value = jnp.concatenate([first, second], 0)
    return value.astype(F32)


def small_sum(value):
    for mask in masks_of(lax.axis_size("narrow")):
        value = value + swap_bit(value, "narrow", mask)
    return value


def norm_forward(summed, gain_row, shift_row):
    row_mean = jnp.mean(summed, axis=-1, keepdims=True)
    centered = summed - row_mean
    variance = jnp.mean(centered * centered, axis=-1, keepdims=True)
    rstd = lax.rsqrt(variance + 1e-12)
    normed = centered * rstd
    return normed * gain_row + shift_row, normed, rstd


def norm_backward(grad, normed, rstd, gain_row):
    upstream = grad * gain_row
    mean_up = jnp.mean(upstream, axis=-1, keepdims=True)
    mean_dot = jnp.mean(upstream * normed, axis=-1, keepdims=True)
    return rstd * (upstream - mean_up - normed * mean_dot)


def gelu_pair(pre):
    cdf = 0.5 * (1.0 + lax.erf(pre * (0.5**0.5)))
    density = jnp.exp(-0.5 * pre * pre) * 0.3989422804014327
    return pre * cdf, cdf + pre * density


def heads_of(rows):
    return rows.reshape(rows.shape[0], -1, HEAD_DIM)


def masked_scores(query, key, page_length):
    scores = jnp.einsum(
        "qhe,khe->hqk", heads_of(query), heads_of(key), preferred_element_type=F32
    ) * HEAD_DIM ** (-0.5)
    valid = jnp.arange(key.shape[0], dtype=jnp.int32) < page_length
    return jnp.where(valid[None, None, :], scores, -1e30)


def attention_forward(query, key, value, page_length):
    masked = masked_scores(query, key, page_length)
    row_max = jnp.max(masked, axis=-1, keepdims=True)
    exponent = jnp.exp(masked - row_max)
    row_total = jnp.sum(exponent, axis=-1, keepdims=True)
    attend_low = (exponent / row_total).astype(B16)
    mixed = jnp.einsum("hqk,khe->qhe", attend_low, heads_of(value), preferred_element_type=F32)
    return mixed.reshape(query.shape).astype(B16), row_max + jnp.log(row_total)


def attention_backward(query, key, value, page_length, log_total, grad_mixed):
    attend = jnp.exp(masked_scores(query, key, page_length) - log_total)
    grad_heads = heads_of(grad_mixed)
    grad_value = jnp.einsum(
        "hqk,qhe->khe", attend.astype(B16), grad_heads, preferred_element_type=F32
    )
    grad_attend = jnp.einsum("qhe,khe->hqk", grad_heads, heads_of(value), preferred_element_type=F32)
    row_dot = jnp.sum(attend * grad_attend, axis=-1, keepdims=True)
    grad_scores = (attend * (grad_attend - row_dot)).astype(B16)
    grad_query = jnp.einsum(
        "hqk,khe->qhe", grad_scores, heads_of(key), preferred_element_type=F32
    ) * HEAD_DIM ** (-0.5)
    grad_key = jnp.einsum(
        "hqk,qhe->khe", grad_scores, heads_of(query), preferred_element_type=F32
    ) * HEAD_DIM ** (-0.5)
    return [g.reshape(query.shape).astype(B16) for g in (grad_query, grad_key, grad_value)]


def local(
    tokens,
    page_len,
    w_qkv,
    b_qv,
    w_out,
    b_out,
    gain_attn,
    shift_attn,
    w_up,
    b_up,
    w_down,
    b_down,
    gain_ffn,
    shift_ffn,
    cotangent,
):
    tok_count, width = tokens.shape
    page_count = page_len.shape[0]
    page_size = tok_count // page_count
    local_width = w_qkv.shape[2]
    local_hidden = w_up.shape[1]
    core = lax.axis_index("wide") % 2
    pages = page_count // 2
    rows = tok_count // 2

    def swap(value):
        return swap_bit(value, "wide", 1)

    def both_cores(mine):
        came = swap(mine)
        return jnp.concatenate([jnp.where(core == 0, mine, came), jnp.where(core == 0, came, mine)], 0)

    own_tokens = lax.dynamic_slice_in_dim(tokens, core * rows, rows, 0)
    own_cot = lax.dynamic_slice_in_dim(cotangent, core * rows, rows, 0)
    own_len = lax.dynamic_slice_in_dim(page_len, core * pages, pages, 0)

    small = jnp.concatenate([b_qv.reshape(-1), b_up])
    small_came = swap(small)
    w_qkv = (w_qkv, swap(w_qkv))
    b_qv = (b_qv, small_came[: 2 * local_width].reshape(2, local_width))
    b_up = (b_up, small_came[2 * local_width :])
    w_out = (w_out, swap(w_out))
    w_up = (w_up, swap(w_up))
    w_down = (w_down, swap(w_down))
    sides = (0, 1)

    qkv = []
    for s in sides:
        biases = (b_qv[s][0], None, b_qv[s][1])
        heads = []
        for c in range(3):
            projected = mm(own_tokens, w_qkv[s][c])
            if biases[c] is not None:
                projected = projected + biases[c]
            heads.append(projected.astype(B16))
        qkv.append(heads)
    step = page_size // CHUNKS
    spans = [(p, p * page_size + k * step) for p in range(pages) for k in range(CHUNKS)]

    mixed, log_total, attn_rows = {}, {}, []
    for page, start in spans:
        keys = slice(page * page_size, (page + 1) * page_size)
        part = 0.0
        for s in sides:
            query, key, value = qkv[s]
            mixed[s, start], log_total[s, start] = attention_forward(
                query[start : start + step], key[keys], value[keys], own_len[page]
            )
            part = part + mm(mixed[s, start], w_out[s])
        attn_rows.append(outer_sum(part))

    hidden, hidden_low, normed_one, rstd_one = [], [], [], []
    active, slope, down_rows = {}, {}, []
    for i, (page, start) in enumerate(spans):
        summed = attn_rows[i] + b_out + own_tokens[start : start + step].astype(F32)
        h, n, r = norm_forward(summed, gain_attn, shift_attn)
        hidden.append(h)
        hidden_low.append(h.astype(B16))
        normed_one.append(n)
        rstd_one.append(r)
        part = 0.0
        for s in sides:
            act, slo = gelu_pair(mm(hidden_low[i], w_up[s]) + b_up[s])
            active[s, i], slope[s, i] = act.astype(B16), slo
            part = part + mm(active[s, i], w_down[s])
        down_rows.append(outer_sum(part))

    out_rows, grad_two, grad_two_low, hidden_rows = [], [], [], []
    gain_two, grad_upper = [], {}
    for i, (page, start) in enumerate(spans):
        out, normed, rstd = norm_forward(down_rows[i] + b_down + hidden[i], gain_ffn, shift_ffn)
        out_rows.append(out.astype(B16))
        cot = own_cot[start : start + step].astype(F32)
        gain_two.append(jnp.sum(cot * normed, axis=0))
        g = norm_backward(cot, normed, rstd, gain_ffn)
        grad_two.append(g)
        grad_two_low.append(g.astype(B16))
        part = 0.0
        for s in sides:
            grad_active = mm_nt(grad_two_low[i], w_down[s])
            grad_upper[s, i] = (grad_active * slope[s, i]).astype(B16)
            part = part + mm_nt(grad_upper[s, i], w_up[s])
        hidden_rows.append(outer_sum(part))

    def join(parts):
        return jnp.concatenate(parts, 0)

    index = range(len(spans))
    grad_two_all = join(grad_two_low)
    down_w = [mm_tn(join([active[s, i] for i in index]), grad_two_all) for s in sides]
    hidden_all = join(hidden_low)
    upper_all = [join([grad_upper[s, i] for i in index]) for s in sides]
    up_w = [mm_tn(hidden_all, upper_all[s]) for s in sides]

    def core_sum(pair):
        return (pair[0] + swap(pair[1].astype(B16)).astype(F32)).astype(B16)

    grad_down_w = narrow_sum(core_sum(down_w))
    grad_up_w = narrow_sum(core_sum(up_w))
    layer_out = both_cores(join(out_rows))

    grad_one, gain_one, grad_one_low = [], [], []
    hidden_grads = []
    for i, (page, start) in enumerate(spans):
        hidden_grad = hidden_rows[i] + grad_two[i]
        hidden_grads.append(hidden_grad)
        gain_one.append(jnp.sum(hidden_grad * normed_one[i], axis=0))
        g = norm_backward(hidden_grad, normed_one[i], rstd_one[i], gain_attn)
        grad_one.append(g)
        grad_one_low.append(g.astype(B16))
    grad_one_all = join(grad_one_low)
    mixed_all = [join([mixed[s, start] for _, start in spans]) for s in sides]
    out_w = [mm_tn(mixed_all[s], grad_one_all) for s in sides]

    grad_qkv = []
    for s in sides:
        query, key, value = qkv[s]
        grads = []
        for page in range(pages):
            keys = slice(page * page_size, (page + 1) * page_size)
            grad_mixed = mm_nt(grad_one_all[keys], w_out[s]).astype(B16)
            logs = jnp.concatenate([log_total[s, start] for p, start in spans if p == page], 1)
            grads.append(
                attention_backward(query[keys], key[keys], value[keys], own_len[page], logs, grad_mixed)
            )
        grad_qkv.append([join([g[c] for g in grads]) for c in range(3)])

    part = 0.0
    for s in sides:
        for c in range(3):
            part = part + mm_nt(grad_qkv[s][c], w_qkv[s][c])
    grad_tokens = (join(grad_one) + outer_sum(part)).astype(B16)
    grad_tokens = both_cores(grad_tokens)

    qkv_w = [
        jnp.concatenate([mm_tn(own_tokens, grad_qkv[s][c]) for c in range(3)], 0) for s in sides
    ]
    grad_qkv_w = narrow_sum(core_sum(qkv_w)).reshape(3, width, local_width)
    grad_out_w = narrow_sum(core_sum(out_w))

    def rows_sum(parts):
        return sum(jnp.sum(part.astype(F32), axis=0) for part in parts)

    shared = [
        rows_sum(grad_one),
        sum(gain_one),
        rows_sum(hidden_grads),
        rows_sum(grad_two),
        sum(gain_two),
        rows_sum([own_cot]),
    ]
    split = [
        jnp.concatenate(
            [rows_sum([upper_all[s]]), rows_sum([grad_qkv[s][0]]), rows_sum([grad_qkv[s][2]])]
        )
        for s in sides
    ]
    shared = jnp.concatenate(shared)
    sent = jnp.concatenate([shared, split[1]])
    vectors = small_sum(jnp.concatenate([shared, split[0]]) + swap(sent))
    six = vectors[: 6 * width].reshape(6, width)
    rest = vectors[6 * width :]
    grad_up_bias = rest[:local_hidden]
    grad_qv_bias = rest[local_hidden:].reshape(2, local_width)
    return (
        layer_out,
        grad_tokens,
        grad_qkv_w,
        grad_qv_bias,
        grad_out_w,
        six[0],
        six[1],
        six[2],
        grad_up_w,
        grad_up_bias,
        grad_down_w,
        six[3],
        six[4],
        six[5],
    )


def solution(mesh):
    placed = (
        P("narrow", None),
        P("narrow"),
        P(None, None, "wide"),
        P(None, "wide"),
        P("wide", None),
        P(),
        P(),
        P(),
        P(None, "wide"),
        P("wide"),
        P("wide", None),
        P(),
        P(),
        P(),
        P("narrow", None),
    )
    return jax.shard_map(
        local,
        mesh=mesh,
        in_specs=placed,
        out_specs=(
            P("narrow", None),
            P("narrow", None),
            P(None, None, "wide"),
            P(None, "wide"),
            P("wide", None),
            P(),
            P(),
            P(),
            P(None, "wide"),
            P("wide"),
            P("wide", None),
            P(),
            P(),
            P(),
        ),
        check_vma=False,
    )
```

```python
import functools

import jax
import jax.numpy as jnp
from jax import lax
from jax.experimental import pallas as pl
from jax.experimental.pallas import tpu as pltpu
from jax.sharding import PartitionSpec as P

HEAD_DIM = 64
CHUNKS = 2
BLOCK = 32

F32 = jnp.float32
B16 = jnp.bfloat16


ANY = pl.BlockSpec(memory_space=pl.ANY)


def dot(a, b, dims):
    return lax.dot_general(a, b, (dims, ((), ())), preferred_element_type=F32)


def mm(a, b):
    return dot(a, b, ((1,), (0,)))


def mm_nt(a, b):
    return dot(a, b, ((1,), (1,)))


def mm_tn(a, b):
    return dot(a, b, ((0,), (0,)))


def shape(dims, dtype):
    return jax.ShapeDtypeStruct(tuple(dims), dtype)


def whole(array):
    zeros = (0,) * len(array.shape)
    return pl.BlockSpec(array.shape, lambda *_: zeros)


def rows_at(array, size, place):
    return pl.BlockSpec((size, array.shape[1]), lambda *_: (place, 0))


def call(body, name, core, ins, outs, aliases=None, scratch=(), grid=(1,), flops=0):
    moved = sum(a.size * a.dtype.itemsize for a, _ in ins)
    moved += sum(o.size * o.dtype.itemsize for o, _ in outs)
    return pl.pallas_call(
        body,
        name=name,
        grid_spec=pltpu.PrefetchScalarGridSpec(
            num_scalar_prefetch=1,
            grid=grid,
            in_specs=[spec for _, spec in ins],
            out_specs=[spec for _, spec in outs],
            scratch_shapes=list(scratch),
        ),
        out_shape=[o for o, _ in outs],
        input_output_aliases={k + 1: v for k, v in (aliases or {}).items()},
        compiler_params=pltpu.CompilerParams(vmem_limit_bytes=48 * 2**20),
        cost_estimate=pl.CostEstimate(flops=flops, bytes_accessed=moved, transcendentals=0),
    )(core, *[a for a, _ in ins])


def project_body(core, tok, w, bias, out):
    out[0] = (mm(tok[...], w[0]) + bias[0]).astype(B16)


def head_masks(width):
    lanes = lax.broadcasted_iota(jnp.int32, (1, width), 1) // HEAD_DIM
    return [lanes == h for h in range(width // HEAD_DIM)]


def attend_body(start, step, core, lens, qkv_own, qkv_peer, out_own, out_peer, *rest):
    mixed_refs, lse, part = rest[-4:-2], rest[-2], rest[-1]
    length = lens[core[0]]
    total = None
    for s, (qkv, w_out) in enumerate(((qkv_own, out_own), (qkv_peer, out_peer))):
        keys, width = qkv.shape[1], qkv.shape[2]
        query = qkv[0, start : start + step, :] * jnp.asarray(HEAD_DIM**-0.5, B16)
        key = qkv[1]
        value_t = qkv[2].astype(F32).T.astype(B16)
        valid = lax.broadcasted_iota(jnp.int32, (keys, step), 0) < length
        mixed = []
        for h, mask in enumerate(head_masks(width)):
            query_h = jnp.where(mask, query, jnp.zeros_like(query))
            scores = jnp.where(valid, mm_nt(key, query_h), -1e30)
            top = jnp.max(scores, axis=0, keepdims=True)
            weights = jnp.exp(scores - top)
            norm = jnp.sum(weights, axis=0, keepdims=True)
            attend = (weights * (1.0 / norm)).astype(B16)
            row = s * (width // HEAD_DIM) + h
            lse[row : row + 1, :] = top + jnp.log(norm)
            mixed.append(mm(value_t[h * HEAD_DIM : (h + 1) * HEAD_DIM], attend))
        low = jnp.concatenate(mixed, 0).T.astype(B16)
        mixed_refs[s][...] = low
        product = mm(low, w_out[...])
        total = product if total is None else total + product
    part[...] = total.astype(B16)


def norm_stats(summed):
    mean = jnp.mean(summed, axis=-1, keepdims=True)
    centered = summed - mean
    variance = jnp.mean(centered * centered, axis=-1, keepdims=True)
    rstd = lax.rsqrt(variance + 1e-12)
    return centered * rstd, rstd


def norm_backward(grad, normed, rstd, gain):
    upstream = grad * gain
    mean_up = jnp.mean(upstream, axis=-1, keepdims=True)
    mean_dot = jnp.mean(upstream * normed, axis=-1, keepdims=True)
    return rstd * (upstream - mean_up - normed * mean_dot)


def row_blocks(count, body):
    def step(i, carry):
        body(pl.ds(pl.multiple_of(i * BLOCK, BLOCK), BLOCK))
        return carry

    lax.fori_loop(0, count // BLOCK, step, 0)


def weight_tiles(pairs, tile, axis, scratch, sems, first):
    waits = []
    for weight in pairs:
        for j in range(weight.shape[axis] // tile):
            at = (slice(None), pl.ds(j * tile, tile)) if axis == 1 else (pl.ds(j * tile, tile),)
            number = len(waits)
            waits.append(
                pltpu.make_async_copy(weight.at[at], scratch.at[number], sems.at[first + number])
            )
    return waits


def ffn_forward_body(
    tile, core, mine, came, tok, b_out, gain, shift, b_up, up_own, up_peer, down_own, down_peer, *rest
):
    hidden_low, act_own, act_peer, normed, rstd, slope, part, up_buf, down_buf, pre_buf, sems = rest[-11:]
    tiles = up_buf.shape[0]
    ups = weight_tiles((up_own, up_peer), tile, 1, up_buf, sems, 0)
    downs = weight_tiles((down_own, down_peer), tile, 0, down_buf, sems, tiles)
    for up, down in zip(ups, downs):
        up.start()
        down.start()
    rows = mine.shape[0]

    def norm_block(at):
        summed = mine[at, :].astype(F32) + came[at, :].astype(F32) + b_out[...] + tok[at, :].astype(F32)
        z, r = norm_stats(summed)
        normed[at, :] = z
        rstd[at, :] = jnp.broadcast_to(r, (BLOCK, 128))
        hidden_low[at, :] = (z * gain[...] + shift[...]).astype(B16)

    row_blocks(rows, norm_block)
    per_side = tiles // 2
    total = None
    for t in range(tiles):
        act = (act_own, act_peer)[t // per_side]
        col = (t % per_side) * tile
        ups[t].wait()
        pre_buf[...] = mm(hidden_low[...], up_buf[t]) + b_up[:, t * tile : (t + 1) * tile]

        def gelu_block(at, act=act, col=col, t=t):
            pre = pre_buf[at, :]
            cdf = 0.5 * (1.0 + lax.erf(pre * (0.5**0.5)))
            density = jnp.exp(-0.5 * pre * pre) * 0.3989422804014327
            act[at, col : col + tile] = (pre * cdf).astype(B16)
            slope[at, t * tile : (t + 1) * tile] = (cdf + pre * density).astype(B16)

        row_blocks(rows, gelu_block)
        downs[t].wait()
        product = mm(act[:, col : col + tile], down_buf[t])
        total = product if total is None else total + product
    part[...] = total.astype(B16)


def second_norm_body(core, mine, came, normed, cot, b_down, gain_attn, shift_attn, gain, shift, *rest):
    out, grad_low, grad_two, stats = rest[-4:]
    stats[...] = jnp.zeros_like(stats)

    def block(at):
        hidden = normed[at, :] * gain_attn[...] + shift_attn[...]
        summed = mine[at, :].astype(F32) + came[at, :].astype(F32) + b_down[...] + hidden
        z, r = norm_stats(summed)
        out[at, :] = (z * gain[...] + shift[...]).astype(B16)
        upper = cot[at, :].astype(F32)
        grad = norm_backward(upper, z, r, gain[...])
        grad_two[at, :] = grad
        grad_low[at, :] = grad.astype(B16)
        stats[0:1, :] += jnp.sum(grad, axis=0, keepdims=True)
        stats[1:2, :] += jnp.sum(upper * z, axis=0, keepdims=True)
        stats[2:3, :] += jnp.sum(upper, axis=0, keepdims=True)

    row_blocks(mine.shape[0], block)


def ffn_backward_body(tile, core, grad_low, slope, up_own, up_peer, down_own, down_peer, *rest):
    upper_own, upper_peer, part, bias, up_buf, down_buf, sems = rest[-7:]
    tiles = up_buf.shape[0]
    ups = weight_tiles((up_own, up_peer), tile, 1, up_buf, sems, 0)
    downs = weight_tiles((down_own, down_peer), tile, 0, down_buf, sems, tiles)
    for up, down in zip(ups, downs):
        down.start()
        up.start()
    per_side = tiles // 2
    total = None
    for t in range(tiles):
        upper_ref = (upper_own, upper_peer)[t // per_side]
        col = (t % per_side) * tile
        downs[t].wait()
        upper = mm_nt(grad_low[...], down_buf[t]) * slope[:, t * tile : (t + 1) * tile].astype(F32)
        low = upper.astype(B16)
        upper_ref[:, col : col + tile] = low
        bias[0:1, t * tile : (t + 1) * tile] = jnp.sum(low.astype(F32), axis=0, keepdims=True)
        ups[t].wait()
        product = mm_nt(low, up_buf[t])
        total = product if total is None else total + product
    part[...] = total.astype(B16)


def first_norm_body(core, mine, came, grad_two, normed, rstd, gain, out_own, out_peer, *rest):
    grad_low, mixed_own, mixed_peer, grad_one, stats = rest[-5:]
    stats[...] = jnp.zeros_like(stats)

    def block(at):
        upper = mine[at, :].astype(F32) + came[at, :].astype(F32) + grad_two[at, :]
        z = normed[at, :]
        grad = norm_backward(upper, z, rstd[at, 0:1], gain[...])
        grad_one[at, :] = grad
        grad_low[at, :] = grad.astype(B16)
        stats[0:1, :] += jnp.sum(grad, axis=0, keepdims=True)
        stats[1:2, :] += jnp.sum(upper * z, axis=0, keepdims=True)
        stats[2:3, :] += jnp.sum(upper, axis=0, keepdims=True)

    row_blocks(mine.shape[0], block)
    mixed_own[...] = mm_nt(grad_low[...], out_own[...]).astype(B16)
    mixed_peer[...] = mm_nt(grad_low[...], out_peer[...]).astype(B16)


def attend_backward_body(
    core, lens, qkv_own, qkv_peer, lse, mixed_own, mixed_peer, grad_own, grad_peer,
    out_own, out_peer, bias, attend_buf, score_buf, query_buf, grad_buf,
):
    length = lens[core[0]]
    scale = jnp.asarray(HEAD_DIM**-0.5, B16)
    rows, width = grad_own.shape
    heads = width // HEAD_DIM
    step = rows // CHUNKS
    masks = head_masks(width)
    picks = lax.broadcasted_iota(jnp.int32, (16, width), 0) == (
        lax.broadcasted_iota(jnp.int32, (16, width), 1) // HEAD_DIM
    )
    picks = jnp.where(picks, 1.0, 0.0).astype(B16)
    sides = ((qkv_own, mixed_own, grad_own, out_own), (qkv_peer, mixed_peer, grad_peer, out_peer))
    for s, (qkv, mixed, grad, out) in enumerate(sides):
        key, value = qkv[1], qkv[2]
        key_t = key.astype(F32).T.astype(B16)
        valid = lax.broadcasted_iota(jnp.int32, (key.shape[0], step), 0) < length
        products = grad[...].astype(F32) * mixed[...].astype(F32)
        high = products.astype(B16)
        dots = mm_nt(picks, high) + mm_nt(picks, (products - high.astype(F32)).astype(B16))
        query_grads = []
        for c in range(CHUNKS):
            span = slice(c * step, (c + 1) * step)
            query = qkv[0, span, :] * scale
            upper = grad[span, :]
            parts = []
            for h, mask in enumerate(masks):
                place = c * heads + h
                at = slice(place * step, (place + 1) * step)
                row = s * heads + h
                query_h = jnp.where(mask, query, jnp.zeros_like(query))
                upper_h = jnp.where(mask, upper, jnp.zeros_like(upper))
                query_buf[at, :] = query_h
                grad_buf[at, :] = upper_h
                scores = mm_nt(key, query_h) - lse[row : row + 1, span]
                attend = jnp.exp(jnp.where(valid, scores, -1e30))
                attend_buf[:, at] = attend.astype(B16)
                grad_attend = mm_nt(value, upper_h)
                grad_scores = (attend * (grad_attend - dots[h : h + 1, span])).astype(B16)
                score_buf[:, at] = grad_scores
                parts.append(mm(key_t[h * HEAD_DIM : (h + 1) * HEAD_DIM], grad_scores))
            query_grads.append(jnp.concatenate(parts, 0).T)
        query_grad = (jnp.concatenate(query_grads, 0) * HEAD_DIM**-0.5).astype(B16)
        key_grad = mm(score_buf[...], query_buf[...]).astype(B16)
        value_grad = mm(attend_buf[...], grad_buf[...]).astype(B16)
        out[0] = query_grad
        out[1] = key_grad
        out[2] = value_grad
        bias[2 * s : 2 * s + 1, :] = jnp.sum(query_grad.astype(F32), axis=0, keepdims=True)
        bias[2 * s + 1 : 2 * s + 2, :] = jnp.sum(value_grad.astype(F32), axis=0, keepdims=True)


def input_body(core, grad_own, grad_peer, w_own, w_peer, part):
    total = None
    for grad, w in ((grad_own, w_own), (grad_peer, w_peer)):
        for c in range(3):
            product = mm_nt(grad[c], w[c])
            total = product if total is None else total + product
    part[...] = total.astype(B16)


def swap_bit(value, axis, mask):
    size = lax.axis_size(axis)
    return lax.ppermute(value, axis, [(i, i ^ mask) for i in range(size)])


def masks_of(size):
    return [1 << k for k in range(size.bit_length() - 1)]


def outer_pair(low, name):
    came = None
    with jax.named_scope(name):
        for mask in masks_of(lax.axis_size("wide"))[1:]:
            if came is not None:
                low = (low.astype(F32) + came.astype(F32)).astype(B16)
            came = swap_bit(low, "wide", mask)
    return low, came


def narrow_sum(value, name):
    masks = masks_of(lax.axis_size("narrow"))
    index = lax.axis_index("narrow")
    bits = [(index // mask) % 2 for mask in masks]
    for k, (mask, bit) in enumerate(zip(masks, bits)):
        half = value.shape[0] // 2
        send = lax.dynamic_slice_in_dim(value, (1 - bit) * half, half, 0)
        keep = lax.dynamic_slice_in_dim(value, bit * half, half, 0)
        with jax.named_scope(f"{name}_rs{k}"):
            came = swap_bit(send, "narrow", mask)
        value = (keep.astype(F32) + came.astype(F32)).astype(B16)
    for k, (mask, bit) in reversed(list(enumerate(zip(masks, bits)))):
        with jax.named_scope(f"{name}_ag{k}"):
            came = swap_bit(value, "narrow", mask)
        first = jnp.where(bit == 0, value, came)
        second = jnp.where(bit == 0, came, value)
        value = jnp.concatenate([first, second], 0)
    return value.astype(F32)


def small_sum(value):
    for mask in masks_of(lax.axis_size("narrow")):
        value = value + swap_bit(value, "narrow", mask)
    return value


def local(
    tokens,
    page_len,
    w_qkv,
    b_qv,
    w_out,
    b_out,
    gain_attn,
    shift_attn,
    w_up,
    b_up,
    w_down,
    b_down,
    gain_ffn,
    shift_ffn,
    cotangent,
):
    tok_count, width = tokens.shape
    page_count = page_len.shape[0]
    page_size = tok_count // page_count
    local_width = w_qkv.shape[2]
    local_hidden = w_up.shape[1]
    heads = 2 * local_width // HEAD_DIM
    core = lax.axis_index("wide") % 2
    assert page_count == 2
    rows = page_size
    step = rows // CHUNKS
    tile = min(512, local_hidden)
    tiles = 2 * local_hidden // tile
    scalar = core.astype(jnp.int32).reshape(1)

    def swap(value, name):
        with jax.named_scope(name):
            return swap_bit(value, "wide", 1)

    def both_cores(mine, name):
        came = swap(mine, name)
        return jnp.concatenate([jnp.where(core == 0, mine, came), jnp.where(core == 0, came, mine)], 0)

    small = jnp.concatenate([b_qv.reshape(-1), b_up])
    small_came = swap(small, "swap_small")
    w_qkv = (w_qkv, swap(w_qkv, "swap_qkv"))
    b_qv = (b_qv, small_came[: 2 * local_width].reshape(2, local_width))
    b_up = jnp.concatenate([b_up, small_came[2 * local_width :]]).reshape(1, -1)
    w_out = (w_out, swap(w_out, "swap_out"))
    w_up = (w_up, swap(w_up, "swap_up"))
    w_down = (w_down, swap(w_down, "swap_down"))
    b_out, gain_attn, shift_attn, b_down, gain_ffn, shift_ffn = [
        v.reshape(1, width) for v in (b_out, gain_attn, shift_attn, b_down, gain_ffn, shift_ffn)
    ]
    sides = (0, 1)
    lens = (page_len, pl.BlockSpec(memory_space=pltpu.SMEM))

    def page_rows(array, size, k):
        return (array, pl.BlockSpec((size, width), lambda i, core: (core[0] * (rows // size) + k, 0)))

    def full(*arrays):
        return [(a, whole(a)) for a in arrays]

    qkv = []
    for s in sides:
        zero = jnp.zeros((1, local_width), F32)
        bias = jnp.stack([b_qv[s][0:1], zero, b_qv[s][1:2]])
        token_spec = pl.BlockSpec((rows, width), lambda i, core: (core[0], 0))
        qkv.append(
            call(
                project_body,
                f"project_{s}",
                scalar,
                [
                    (tokens, token_spec),
                    (w_qkv[s], pl.BlockSpec((1, width, local_width), lambda i, core: (i, 0, 0))),
                    (bias, pl.BlockSpec((1, 1, local_width), lambda i, core: (i, 0, 0))),
                ],
                [
                    (
                        shape((3, rows, local_width), B16),
                        pl.BlockSpec((1, rows, local_width), lambda i, core: (i, 0, 0)),
                    )
                ],
                grid=(3,),
                flops=6 * rows * width * local_width,
            )[0]
        )

    def paged(shapes, k):
        return [(o, rows_at(o, step, k)) for o in shapes]

    def run(body, name, k, ins, spanning, single, kept, **more):
        ins = list(ins)
        aliases = {}
        if kept is not None:
            for n, array in enumerate(kept):
                aliases[len(ins)] = n
                ins.append((array, ANY))
        outs = spanning + [(o, whole(o)) for o in single]
        return call(body, f"{name}_{k}", scalar, ins, outs, aliases=aliases, **more)

    page_wide = shape((rows, width), B16)
    mixed_shape = shape((rows, local_width), B16)
    lse_shape = shape((heads, rows), F32)
    kept, attn_pairs = None, []
    for k in range(CHUNKS):
        *kept, part = run(
            functools.partial(attend_body, k * step, step),
            "attend",
            k,
            [lens] + full(*qkv, *w_out),
            paged([mixed_shape, mixed_shape], k)
            + [(lse_shape, pl.BlockSpec((heads, step), lambda *_, k=k: (0, k)))],
            [shape((step, width), B16)],
            kept,
            flops=4 * step * width * local_width + 8 * step * rows * local_width,
        )
        attn_pairs.append(outer_pair(part, f"swap_attn_{k}"))
    mixed, lse = kept[:2], kept[2]

    weight_scratch = [
        pltpu.VMEM((tiles, width, tile), B16),
        pltpu.VMEM((tiles, tile, width), B16),
    ]
    weights = [(w, ANY) for w in (*w_up, *w_down)]
    hidden_shape = shape((rows, local_hidden), B16)
    kept, norms, slopes, down_pairs = None, [], [], []
    for k in range(CHUNKS):
        results = run(
            functools.partial(ffn_forward_body, tile),
            "ffn_forward",
            k,
            full(*attn_pairs[k])
            + [page_rows(tokens, step, k)]
            + full(b_out, gain_attn, shift_attn, b_up)
            + weights,
            paged([page_wide, hidden_shape, hidden_shape], k),
            [
                shape((step, width), F32),
                shape((step, 128), F32),
                shape((step, 2 * local_hidden), B16),
                shape((step, width), B16),
            ],
            kept,
            scratch=weight_scratch
            + [pltpu.VMEM((step, tile), F32), pltpu.SemaphoreType.DMA((2 * tiles,))],
            flops=8 * step * width * local_hidden,
        )
        kept = results[:3]
        normed, rstd, slope, part = results[3:]
        norms.append((normed, rstd))
        slopes.append(slope)
        down_pairs.append(outer_pair(part, f"swap_down_rows_{k}"))
    hidden_low, active = kept[0], kept[1:]

    kept_norm, kept_upper, grad_two, stats_two, up_bias, hidden_pairs = None, None, [], [], [], []
    stats_shape = shape((8, width), F32)
    for k in range(CHUNKS):
        *kept_norm, grad, stats = run(
            second_norm_body,
            "second_norm",
            k,
            full(*down_pairs[k], norms[k][0])
            + [page_rows(cotangent, step, k)]
            + full(b_down, gain_attn, shift_attn, gain_ffn, shift_ffn),
            paged([page_wide, page_wide], k),
            [shape((step, width), F32), stats_shape],
            kept_norm,
        )
        grad_two.append(grad)
        stats_two.append(stats)
        *kept_upper, part, bias = run(
            functools.partial(ffn_backward_body, tile),
            "ffn_backward",
            k,
            [(kept_norm[1], rows_at(kept_norm[1], step, k))] + full(slopes[k]) + weights,
            paged([hidden_shape, hidden_shape], k),
            [shape((step, width), B16), shape((8, 2 * local_hidden), F32)],
            kept_upper,
            scratch=weight_scratch + [pltpu.SemaphoreType.DMA((2 * tiles,))],
            flops=8 * step * width * local_hidden,
        )
        up_bias.append(bias)
        hidden_pairs.append(outer_pair(part, f"swap_hidden_{k}"))
    out_rows, grad_two_low = kept_norm

    def weight_grad(pairs, name):
        with jax.named_scope(f"{name}_peer"):
            peer = mm_tn(*pairs[1]).astype(B16)
        came = swap(peer, f"{name}_swap")
        with jax.named_scope(f"{name}_own"):
            return (mm_tn(*pairs[0]) + came.astype(F32)).astype(B16)

    grad_down_w = narrow_sum(weight_grad([(active[s], grad_two_low) for s in sides], "down_w"), "sum_down")
    grad_up_w = narrow_sum(
        weight_grad([(hidden_low, kept_upper[s]) for s in sides], "up_w"), "sum_up"
    )
    layer_out = both_cores(out_rows, "swap_layer_out")

    kept, grad_one, stats_one = None, [], []
    for k in range(CHUNKS):
        results = run(
            first_norm_body,
            "first_norm",
            k,
            full(*hidden_pairs[k], grad_two[k], *norms[k], gain_attn, *w_out),
            paged([page_wide, mixed_shape, mixed_shape], k),
            [shape((step, width), F32), stats_shape],
            kept,
            flops=4 * step * width * local_width,
        )
        kept = results[:3]
        grad_one.append(results[3])
        stats_one.append(results[4])
    grad_one_low, grad_mixed = kept[0], kept[1:]

    stacked = CHUNKS * heads // 2 * step
    *grad_qkv, qv_bias = call(
        attend_backward_body,
        "attend_backward",
        scalar,
        [lens] + full(*qkv, lse, *mixed, *grad_mixed),
        [(o, whole(o)) for o in [shape((3, rows, local_width), B16)] * 2 + [shape((8, local_width), F32)]],
        scratch=[
            pltpu.VMEM((rows, stacked), B16),
            pltpu.VMEM((rows, stacked), B16),
            pltpu.VMEM((stacked, local_width), B16),
            pltpu.VMEM((stacked, local_width), B16),
        ],
        flops=20 * rows * rows * local_width,
    )
    grad_out_w = weight_grad([(mixed[s], grad_one_low) for s in sides], "out_w")

    part = call(
        input_body,
        "input_grad",
        scalar,
        full(*grad_qkv, *w_qkv),
        [(page_wide, whole(page_wide))],
        flops=12 * rows * width * local_width,
    )[0]
    own_tokens = lax.dynamic_slice_in_dim(tokens, core * rows, rows, 0)
    with jax.named_scope("qkv_w_peer"):
        peer = jnp.concatenate([mm_tn(own_tokens, grad_qkv[1][c]).astype(B16) for c in range(3)], 0)
    came = swap(peer, "qkv_w_swap")
    with jax.named_scope("qkv_w_own"):
        own = jnp.concatenate([mm_tn(own_tokens, grad_qkv[0][c]) for c in range(3)], 0)
        grad_qkv_w = (own + came.astype(F32)).astype(B16)
    grad_qkv_w = narrow_sum(grad_qkv_w, "sum_qkv").reshape(3, width, local_width)
    grad_out_w = narrow_sum(grad_out_w, "sum_out")

    low, came = outer_pair(part, "swap_input")
    grad_tokens = (jnp.concatenate(grad_one, 0) + (low.astype(F32) + came.astype(F32))).astype(B16)
    grad_tokens = both_cores(grad_tokens, "swap_grad_tokens")

    one = sum(stats_one)
    two = sum(stats_two)
    up = sum(up_bias)[0].reshape(2, local_hidden)
    qv = qv_bias[:4].reshape(2, 2 * local_width)
    shared = jnp.concatenate([one[:3], two[:3]], 0).reshape(-1)
    mine = jnp.concatenate([shared, up[0], qv[0]])
    sent = jnp.concatenate([shared, up[1], qv[1]])
    vectors = small_sum(mine + swap(sent, "swap_vectors"))
    six = vectors[: 6 * width].reshape(6, width)
    rest = vectors[6 * width :]
    grad_up_bias = rest[:local_hidden]
    grad_qv_bias = rest[local_hidden:].reshape(2, local_width)
    return (
        layer_out,
        grad_tokens,
        grad_qkv_w,
        grad_qv_bias,
        grad_out_w,
        six[0],
        six[1],
        six[2],
        grad_up_w,
        grad_up_bias,
        grad_down_w,
        six[3],
        six[4],
        six[5],
    )


def solution(mesh):
    placed = (
        P("narrow", None),
        P("narrow"),
        P(None, None, "wide"),
        P(None, "wide"),
        P("wide", None),
        P(),
        P(),
        P(),
        P(None, "wide"),
        P("wide"),
        P("wide", None),
        P(),
        P(),
        P(),
        P("narrow", None),
    )
    return jax.shard_map(
        local,
        mesh=mesh,
        in_specs=placed,
        out_specs=(
            P("narrow", None),
            P("narrow", None),
            P(None, None, "wide"),
            P(None, "wide"),
            P("wide", None),
            P(),
            P(),
            P(),
            P(None, "wide"),
            P("wide"),
            P("wide", None),
            P(),
            P(),
            P(),
        ),
        check_vma=False,
    )
```

```python
import functools

import jax
import jax.numpy as jnp
from jax import lax
from jax.experimental import pallas as pl
from jax.experimental.pallas import tpu as pltpu
from jax.sharding import PartitionSpec as P

HEAD_DIM = 64
CHUNKS = 2
BLOCK = 128

F32 = jnp.float32
B16 = jnp.bfloat16


ANY = pl.BlockSpec(memory_space=pl.ANY)

ORDERS = {}


def dot(a, b, dims):
    return lax.dot_general(a, b, (dims, ((), ())), preferred_element_type=F32)


def mm(a, b):
    return dot(a, b, ((1,), (0,)))


def mm_nt(a, b):
    return dot(a, b, ((1,), (1,)))


def mm_tn(a, b):
    return dot(a, b, ((0,), (0,)))


def shape(dims, dtype):
    return jax.ShapeDtypeStruct(tuple(dims), dtype)


def whole(array):
    zeros = (0,) * len(array.shape)
    return pl.BlockSpec(array.shape, lambda *_: zeros)


def rows_at(array, size, place):
    return pl.BlockSpec((size, array.shape[1]), lambda *_: (place, 0))


def call(body, name, core, ins, outs, aliases=None, scratch=(), grid=(1,), flops=0):
    moved = sum(a.size * a.dtype.itemsize for a, _ in ins)
    moved += sum(o.size * o.dtype.itemsize for o, _ in outs)
    kernel = pl.pallas_call(
        body,
        name=name,
        grid_spec=pltpu.PrefetchScalarGridSpec(
            num_scalar_prefetch=1,
            grid=grid,
            in_specs=[spec for _, spec in ins],
            out_specs=[spec for _, spec in outs],
            scratch_shapes=list(scratch),
        ),
        out_shape=[o for o, _ in outs],
        input_output_aliases={k + 1: v for k, v in (aliases or {}).items()},
        compiler_params=pltpu.CompilerParams(vmem_limit_bytes=40 * 2**20),
        cost_estimate=pl.CostEstimate(flops=flops, bytes_accessed=moved, transcendentals=0),
    )
    with jax.named_scope(name):
        return kernel(core, *[a for a, _ in ins])


def project_body(core, tok, w, bias, out):
    out[0] = (mm(tok[...], w[0]) + bias[0]).astype(B16)


def head_masks(width):
    lanes = lax.broadcasted_iota(jnp.int32, (1, width), 1) // HEAD_DIM
    return [lanes == h for h in range(width // HEAD_DIM)]


def attend_body(start, step, core, lens, qkv_own, qkv_peer, out_own, out_peer, *rest):
    mixed_refs, lse, part = rest[-4:-2], rest[-2], rest[-1]
    length = lens[core[0]]
    total = None
    for s, (qkv, w_out) in enumerate(((qkv_own, out_own), (qkv_peer, out_peer))):
        keys, width = qkv.shape[1], qkv.shape[2]
        query = qkv[0, start : start + step, :] * jnp.asarray(HEAD_DIM**-0.5, B16)
        key = qkv[1]
        value_t = qkv[2].astype(F32).T.astype(B16)
        valid = lax.broadcasted_iota(jnp.int32, (keys, step), 0) < length
        mixed = []
        for h, mask in enumerate(head_masks(width)):
            query_h = jnp.where(mask, query, jnp.zeros_like(query))
            scores = jnp.where(valid, mm_nt(key, query_h), -1e30)
            top = jnp.max(scores, axis=0, keepdims=True)
            weights = jnp.exp(scores - top)
            norm = jnp.sum(weights, axis=0, keepdims=True)
            attend = (weights * (1.0 / norm)).astype(B16)
            row = s * (width // HEAD_DIM) + h
            lse[row : row + 1, :] = top + jnp.log(norm)
            mixed.append(mm(value_t[h * HEAD_DIM : (h + 1) * HEAD_DIM], attend))
        low = jnp.concatenate(mixed, 0).T.astype(B16)
        mixed_refs[s][...] = low
        product = mm(low, w_out[...])
        total = product if total is None else total + product
    part[...] = total.astype(B16)


def norm_stats(summed):
    mean = jnp.mean(summed, axis=-1, keepdims=True)
    centered = summed - mean
    variance = jnp.mean(centered * centered, axis=-1, keepdims=True)
    rstd = lax.rsqrt(variance + 1e-12)
    return centered * rstd, rstd


def norm_backward(grad, normed, rstd, gain):
    upstream = grad * gain
    mean_up = jnp.mean(upstream, axis=-1, keepdims=True)
    mean_dot = jnp.mean(upstream * normed, axis=-1, keepdims=True)
    return rstd * (upstream - mean_up - normed * mean_dot)


def row_blocks(count, body):
    def step(i, carry):
        body(pl.ds(pl.multiple_of(i * BLOCK, BLOCK), BLOCK))
        return carry

    lax.fori_loop(0, count // BLOCK, step, 0)


def weight_tiles(pairs, tile, axis, scratch, sems, first):
    waits = []
    for weight in pairs:
        for j in range(weight.shape[axis] // tile):
            at = (slice(None), pl.ds(j * tile, tile)) if axis == 1 else (pl.ds(j * tile, tile),)
            number = len(waits)
            waits.append(
                pltpu.make_async_copy(weight.at[at], scratch.at[number], sems.at[first + number])
            )
    return waits


def ffn_forward_body(
    tile, core, mine, came, tok, b_out, gain, shift, b_up, up_own, up_peer, down_own, down_peer, *rest
):
    hidden_low, act_own, act_peer, normed, rstd, slope, part, up_buf, down_buf, pre_buf, sems = rest[-11:]
    tiles = up_buf.shape[0]
    ups = weight_tiles((up_own, up_peer), tile, 1, up_buf, sems, 0)
    downs = weight_tiles((down_own, down_peer), tile, 0, down_buf, sems, tiles)
    for up, down in zip(ups, downs):
        up.start()
        down.start()
    rows = mine.shape[0]

    def norm_block(at):
        summed = mine[at, :].astype(F32) + came[at, :].astype(F32) + b_out[...] + tok[at, :].astype(F32)
        z, r = norm_stats(summed)
        normed[at, :] = z
        rstd[at, :] = jnp.broadcast_to(r, (BLOCK, 128))
        hidden_low[at, :] = (z * gain[...] + shift[...]).astype(B16)

    row_blocks(rows, norm_block)
    per_side = tiles // 2
    total = None
    for t in range(tiles):
        act = (act_own, act_peer)[t // per_side]
        col = (t % per_side) * tile
        ups[t].wait()
        pre_buf[...] = mm(hidden_low[...], up_buf[t]) + b_up[:, t * tile : (t + 1) * tile]

        def gelu_block(at, act=act, col=col, t=t):
            pre = pre_buf[at, :]
            cdf = 0.5 * (1.0 + lax.erf(pre * (0.5**0.5)))
            density = jnp.exp(-0.5 * pre * pre) * 0.3989422804014327
            act[at, col : col + tile] = (pre * cdf).astype(B16)
            slope[at, t * tile : (t + 1) * tile] = (cdf + pre * density).astype(B16)

        row_blocks(rows, gelu_block)
        downs[t].wait()
        product = mm(act[:, col : col + tile], down_buf[t])
        total = product if total is None else total + product
    part[...] = total.astype(B16)


def second_norm_body(core, mine, came, normed, cot, b_down, gain_attn, shift_attn, gain, shift, *rest):
    out_all, out, grad_low, grad_two, stats = rest[-5:]
    stats[...] = jnp.zeros_like(stats)

    def block(at):
        hidden = normed[at, :] * gain_attn[...] + shift_attn[...]
        summed = mine[at, :].astype(F32) + came[at, :].astype(F32) + b_down[...] + hidden
        z, r = norm_stats(summed)
        result = (z * gain[...] + shift[...]).astype(B16)
        out[at, :] = result
        out_all[at, :] = result
        upper = cot[at, :].astype(F32)
        grad = norm_backward(upper, z, r, gain[...])
        grad_two[at, :] = grad
        grad_low[at, :] = grad.astype(B16)
        for n, value in enumerate((grad, upper * z, upper)):
            stats[n] += jnp.sum(value.reshape(BLOCK // 8, 8, value.shape[1]), axis=0)

    row_blocks(mine.shape[0], block)


def ffn_backward_body(tile, core, grad_low, slope, up_own, up_peer, down_own, down_peer, *rest):
    upper_own, upper_peer, part, bias, up_buf, down_buf, sems = rest[-7:]
    tiles = up_buf.shape[0]
    ups = weight_tiles((up_own, up_peer), tile, 1, up_buf, sems, 0)
    downs = weight_tiles((down_own, down_peer), tile, 0, down_buf, sems, tiles)
    for up, down in zip(ups, downs):
        down.start()
        up.start()
    per_side = tiles // 2
    total = None
    for t in range(tiles):
        upper_ref = (upper_own, upper_peer)[t // per_side]
        col = (t % per_side) * tile
        downs[t].wait()
        upper = mm_nt(grad_low[...], down_buf[t]) * slope[:, t * tile : (t + 1) * tile].astype(F32)
        low = upper.astype(B16)
        upper_ref[:, col : col + tile] = low
        bias[0:1, t * tile : (t + 1) * tile] = jnp.sum(low.astype(F32), axis=0, keepdims=True)
        ups[t].wait()
        product = mm_nt(low, up_buf[t])
        total = product if total is None else total + product
    part[...] = total.astype(B16)


def first_norm_body(core, mine, came, grad_two, normed, rstd, gain, out_own, out_peer, *rest):
    grad_low, mixed_own, mixed_peer, grad_one, stats = rest[-5:]
    stats[...] = jnp.zeros_like(stats)

    def block(at):
        upper = mine[at, :].astype(F32) + came[at, :].astype(F32) + grad_two[at, :]
        z = normed[at, :]
        grad = norm_backward(upper, z, rstd[at, 0:1], gain[...])
        grad_one[at, :] = grad
        grad_low[at, :] = grad.astype(B16)
        for n, value in enumerate((grad, upper * z, upper)):
            stats[n] += jnp.sum(value.reshape(BLOCK // 8, 8, value.shape[1]), axis=0)

    row_blocks(mine.shape[0], block)
    mixed_own[...] = mm_nt(grad_low[...], out_own[...]).astype(B16)
    mixed_peer[...] = mm_nt(grad_low[...], out_peer[...]).astype(B16)


def attend_backward_body(
    first_row, core, lens, qkv, lse, mixed, grad, out, bias, attend_buf, score_buf, query_buf, grad_buf
):
    length = lens[core[0]]
    scale = jnp.asarray(HEAD_DIM**-0.5, B16)
    rows, width = grad.shape
    heads = width // HEAD_DIM
    step = rows // CHUNKS
    masks = head_masks(width)
    picks = lax.broadcasted_iota(jnp.int32, (16, width), 0) == (
        lax.broadcasted_iota(jnp.int32, (16, width), 1) // HEAD_DIM
    )
    picks = jnp.where(picks, 1.0, 0.0).astype(B16)
    key, value = qkv[1], qkv[2]
    key_t = key.astype(F32).T.astype(B16)
    valid = lax.broadcasted_iota(jnp.int32, (key.shape[0], step), 0) < length
    products = grad[...].astype(F32) * mixed[...].astype(F32)
    high = products.astype(B16)
    dots = mm_nt(picks, high) + mm_nt(picks, (products - high.astype(F32)).astype(B16))
    query_grads = []
    for c in range(CHUNKS):
        span = slice(c * step, (c + 1) * step)
        query = qkv[0, span, :] * scale
        upper = grad[span, :]
        parts = []
        for h, mask in enumerate(masks):
            place = c * heads + h
            at = slice(place * step, (place + 1) * step)
            row = first_row + h
            query_h = jnp.where(mask, query, jnp.zeros_like(query))
            upper_h = jnp.where(mask, upper, jnp.zeros_like(upper))
            query_buf[at, :] = query_h
            grad_buf[at, :] = upper_h
            scores = mm_nt(key, query_h) - lse[row : row + 1, span]
            attend = jnp.exp(jnp.where(valid, scores, -1e30))
            attend_buf[:, at] = attend.astype(B16)
            grad_attend = mm_nt(value, upper_h)
            grad_scores = (attend * (grad_attend - dots[h : h + 1, span])).astype(B16)
            score_buf[:, at] = grad_scores
            parts.append(mm(key_t[h * HEAD_DIM : (h + 1) * HEAD_DIM], grad_scores))
        query_grads.append(jnp.concatenate(parts, 0).T)
    query_grad = (jnp.concatenate(query_grads, 0) * HEAD_DIM**-0.5).astype(B16)
    key_grad = mm(score_buf[...], query_buf[...]).astype(B16)
    value_grad = mm(attend_buf[...], grad_buf[...]).astype(B16)
    out[0] = query_grad
    out[1] = key_grad
    out[2] = value_grad
    bias[0:1, :] = jnp.sum(query_grad.astype(F32), axis=0, keepdims=True)
    bias[1:2, :] = jnp.sum(value_grad.astype(F32), axis=0, keepdims=True)


def tokens_body(core, low, came, grad_one_0, grad_one_1, result_all, result):
    at = pl.program_id(0)
    step = low.shape[0]
    grad = jnp.where(at < 2, grad_one_0[...], grad_one_1[...])
    total = (grad + low[...].astype(F32) + came[...].astype(F32)).astype(B16)
    result_all[...] = total
    result[...] = total


def input_body(core, grad_own, grad_peer, w_own, w_peer, part):
    total = None
    for grad, w in ((grad_own, w_own), (grad_peer, w_peer)):
        for c in range(3):
            product = mm_nt(grad[c], w[c])
            total = product if total is None else total + product
    part[...] = total.astype(B16)


def swap_bit(value, axis, mask):
    size = lax.axis_size(axis)
    return lax.ppermute(value, axis, [(i, i ^ mask) for i in range(size)])


def masks_of(size):
    return [1 << k for k in range(size.bit_length() - 1)]


def outer_pair(low, name):
    came = None
    with jax.named_scope(name):
        for mask in masks_of(lax.axis_size("wide"))[1:]:
            if came is not None:
                low = (low.astype(F32) + came.astype(F32)).astype(B16)
            came = swap_bit(low, "wide", mask)
    return low, came


def weight_body(core, *refs):
    a, b, out = refs[0], refs[1], refs[-1]
    product = mm_tn(a[...], b[...] if len(b.shape) == 2 else b[0])
    if len(refs) == 4:
        product = product + refs[2][0].astype(F32)
    out[0] = product.astype(B16)


def split_body(core, keep, came, send, kept):
    total = (keep[...].astype(F32) + came[...].astype(F32)).astype(B16)

    @pl.when(pl.program_id(0) == 0)
    def _():
        send[...] = total

    @pl.when(pl.program_id(0) == 1)
    def _():
        kept[...] = total


def add_body(core, keep, came, out):
    out[...] = (keep[...].astype(F32) + came[...].astype(F32)).astype(B16)


def join_body(place, core, mine, came, out):
    mine_now = pl.program_id(0) == core[place]

    @pl.when(mine_now)
    def _():
        out[...] = mine[...]

    @pl.when(jnp.logical_not(mine_now))
    def _():
        out[...] = came[...]


def widen_body(core, half, *rest):
    out = rest[-1]
    out[...] = half[...].astype(out.dtype)


class NarrowSum:
    def __init__(self, name, order, scalar):
        self.name, self.order, self.scalar = name, order, scalar

    def send(self, value, step, mask):
        with jax.named_scope(f"{self.name}_{step}"):
            return swap_bit(value, "narrow", mask)

    def call(self, body, step, ins, outs, **more):
        return call(body, f"{self.name}_{step}", self.scalar, ins, outs, **more)

    def run(self, send, keep):
        groups, rows, columns = keep.shape
        count = len(self.order)
        for k, mask in enumerate(self.order):
            came = self.send(send, f"rs{k}", mask)
            if k + 1 == count:
                piece = shape((groups, rows, columns), B16)
                keep = self.call(
                    add_body, f"add{k}", [(keep, whole(keep)), (came, whole(came))], [(piece, whole(piece))]
                )[0]
                break
            rows //= 2
            place = 2 * bit_index(self.order[k + 1])
            at = pl.BlockSpec(
                (groups, rows, columns),
                lambda i, info, p=place: (0, jnp.where(i == 0, info[p + 2], info[p + 1]), 0),
            )
            half = shape((groups, rows, columns), B16)
            send, keep = self.call(
                split_body,
                f"add{k}",
                [(keep, at), (came, at)],
                [(half, whole(half)), (half, whole(half))],
                grid=(2,),
            )
        for k in reversed(range(1, count)):
            came = self.send(keep, f"ag{k}", self.order[k])
            place = 2 * bit_index(self.order[k]) + 1
            at = pl.BlockSpec((groups, rows, columns), lambda i, info: (0, i, 0))
            keep = self.call(
                functools.partial(join_body, place),
                f"join{k}",
                [(keep, whole(keep)), (came, whole(came))],
                [(shape((groups, 2 * rows, columns), B16), at)],
                grid=(2,),
            )[0]
            rows *= 2
        came = self.send(keep, "ag0", self.order[0])
        place = 2 * bit_index(self.order[0])
        out = shape((groups, 2 * rows, columns), F32)
        pieces = 4
        blocks = [
            pl.BlockSpec(
                (groups, rows // pieces, columns), lambda i, info, p=p: (0, info[p] * pieces + i, 0)
            )
            for p in (place + 1, place + 2)
        ]
        here = pl.BlockSpec((groups, rows // pieces, columns), lambda i, info: (0, i, 0))
        result = self.call(widen_body, "mine", [(keep, here)], [(out, blocks[0])], grid=(pieces,))[0]
        return self.call(
            widen_body,
            "came",
            [(came, here), (result, ANY)],
            [(out, blocks[1])],
            aliases={1: 0},
            grid=(pieces,),
        )[0]


def bit_index(mask):
    return mask.bit_length() - 1


def plain_narrow_sum(value):
    masks = masks_of(lax.axis_size("narrow"))
    for mask in masks:
        came = swap_bit(value, "narrow", mask)
        value = (value.astype(F32) + came.astype(F32)).astype(B16)
    return value.astype(F32)


def small_sum(value):
    for mask in masks_of(lax.axis_size("narrow")):
        with jax.named_scope(f"vectors_{bit_index(mask)}"):
            value = value + swap_bit(value, "narrow", mask)
    return value


def local(
    tokens,
    page_len,
    w_qkv,
    b_qv,
    w_out,
    b_out,
    gain_attn,
    shift_attn,
    w_up,
    b_up,
    w_down,
    b_down,
    gain_ffn,
    shift_ffn,
    cotangent,
):
    tok_count, width = tokens.shape
    page_count = page_len.shape[0]
    page_size = tok_count // page_count
    local_width = w_qkv.shape[2]
    local_hidden = w_up.shape[1]
    heads = 2 * local_width // HEAD_DIM
    core = lax.axis_index("wide") % 2
    assert page_count == 2
    rows = page_size
    step = rows // CHUNKS
    tile = min(512, local_hidden)
    tiles = 2 * local_hidden // tile
    masks = masks_of(lax.axis_size("narrow"))
    bits = [(lax.axis_index("narrow") // mask) % 2 for mask in masks]
    scalar = jnp.stack([core] + [b for bit in bits for b in (bit, 1 - bit)]).astype(jnp.int32)

    def swap(value, name):
        with jax.named_scope(name):
            return swap_bit(value, "wide", 1)

    small = jnp.concatenate([b_qv.reshape(-1), b_up])
    small_came = swap(small, "swap_small")
    w_qkv = (w_qkv, swap(w_qkv, "swap_qkv"))
    b_qv = (b_qv, small_came[: 2 * local_width].reshape(2, local_width))
    b_up = jnp.concatenate([b_up, small_came[2 * local_width :]]).reshape(1, -1)
    w_out = (w_out, swap(w_out, "swap_out"))
    w_up = (w_up, swap(w_up, "swap_up"))
    w_down = (w_down, swap(w_down, "swap_down"))
    b_out, gain_attn, shift_attn, b_down, gain_ffn, shift_ffn = [
        v.reshape(1, width) for v in (b_out, gain_attn, shift_attn, b_down, gain_ffn, shift_ffn)
    ]
    sides = (0, 1)
    lens = (page_len, pl.BlockSpec(memory_space=pltpu.SMEM))

    def page_rows(array, size, k):
        return (array, pl.BlockSpec((size, width), lambda i, core: (core[0] * (rows // size) + k, 0)))

    def full(*arrays):
        return [(a, whole(a)) for a in arrays]

    qkv = []
    for s in sides:
        zero = jnp.zeros((1, local_width), F32)
        bias = jnp.stack([b_qv[s][0:1], zero, b_qv[s][1:2]])
        token_spec = pl.BlockSpec((rows, width), lambda i, core: (core[0], 0))
        qkv.append(
            call(
                project_body,
                f"project_{s}",
                scalar,
                [
                    (tokens, token_spec),
                    (w_qkv[s], pl.BlockSpec((1, width, local_width), lambda i, core: (i, 0, 0))),
                    (bias, pl.BlockSpec((1, 1, local_width), lambda i, core: (i, 0, 0))),
                ],
                [
                    (
                        shape((3, rows, local_width), B16),
                        pl.BlockSpec((1, rows, local_width), lambda i, core: (i, 0, 0)),
                    )
                ],
                grid=(3,),
                flops=6 * rows * width * local_width,
            )[0]
        )

    def paged(shapes, k):
        return [(o, rows_at(o, step, k)) for o in shapes]

    def run(body, name, k, ins, spanning, single, kept, **more):
        ins = list(ins)
        aliases = {}
        if kept is not None:
            for n, array in enumerate(kept):
                aliases[len(ins)] = n
                ins.append((array, ANY))
        outs = spanning + [(o, whole(o)) for o in single]
        return call(body, f"{name}_{k}", scalar, ins, outs, aliases=aliases, **more)

    page_wide = shape((rows, width), B16)
    mixed_shape = shape((rows, local_width), B16)
    lse_shape = shape((heads, rows), F32)
    kept, attn_pairs = None, []
    for k in range(CHUNKS):
        *kept, part = run(
            functools.partial(attend_body, k * step, step),
            "attend",
            k,
            [lens] + full(*qkv, *w_out),
            paged([mixed_shape, mixed_shape], k)
            + [(lse_shape, pl.BlockSpec((heads, step), lambda *_, k=k: (0, k)))],
            [shape((step, width), B16)],
            kept,
            flops=4 * step * width * local_width + 8 * step * rows * local_width,
        )
        attn_pairs.append(outer_pair(part, f"swap_attn_{k}"))
    mixed, lse = kept[:2], kept[2]

    weight_scratch = [
        pltpu.VMEM((tiles, width, tile), B16),
        pltpu.VMEM((tiles, tile, width), B16),
    ]
    weights = [(w, ANY) for w in (*w_up, *w_down)]
    hidden_shape = shape((rows, local_hidden), B16)
    kept, norms, slopes, down_pairs = None, [], [], []
    for k in range(CHUNKS):
        results = run(
            functools.partial(ffn_forward_body, tile),
            "ffn_forward",
            k,
            full(*attn_pairs[k])
            + [page_rows(tokens, step, k)]
            + full(b_out, gain_attn, shift_attn, b_up)
            + weights,
            paged([page_wide, hidden_shape, hidden_shape], k),
            [
                shape((step, width), F32),
                shape((step, 128), F32),
                shape((step, 2 * local_hidden), B16),
                shape((step, width), B16),
            ],
            kept,
            scratch=weight_scratch
            + [pltpu.VMEM((step, tile), F32), pltpu.SemaphoreType.DMA((2 * tiles,))],
            flops=8 * step * width * local_hidden,
        )
        kept = results[:3]
        normed, rstd, slope, part = results[3:]
        norms.append((normed, rstd))
        slopes.append(slope)
        down_pairs.append(outer_pair(part, f"swap_down_rows_{k}"))
    hidden_low, active = kept[0], kept[1:]

    kept_norm, kept_upper, grad_two, stats_two, up_bias, hidden_pairs = None, None, [], [], [], []
    stats_shape = shape((3, 8, width), F32)
    for k in range(CHUNKS):
        *kept_norm, grad, stats = run(
            second_norm_body,
            "second_norm",
            k,
            full(*down_pairs[k], norms[k][0])
            + [page_rows(cotangent, step, k)]
            + full(b_down, gain_attn, shift_attn, gain_ffn, shift_ffn),
            [(shape((tok_count, width), B16), page_rows(tokens, step, k)[1])]
            + paged([page_wide, page_wide], k),
            [shape((step, width), F32), stats_shape],
            kept_norm,
        )
        grad_two.append(grad)
        stats_two.append(stats)
        *kept_upper, part, bias = run(
            functools.partial(ffn_backward_body, tile),
            "ffn_backward",
            k,
            [(kept_norm[2], rows_at(kept_norm[2], step, k))] + full(slopes[k]) + weights,
            paged([hidden_shape, hidden_shape], k),
            [shape((step, width), B16), shape((8, 2 * local_hidden), F32)],
            kept_upper,
            scratch=weight_scratch + [pltpu.SemaphoreType.DMA((2 * tiles,))],
            flops=8 * step * width * local_hidden,
        )
        up_bias.append(bias)
        hidden_pairs.append(outer_pair(part, f"swap_hidden_{k}"))
    layer_out, out_rows, grad_two_low = kept_norm

    def place_partner(result, mine, name):
        came = swap(mine, f"swap_{name}")
        quarter = rows // 4
        return call(
            widen_body,
            f"place_{name}",
            scalar,
            [(came, pl.BlockSpec((quarter, width), lambda i, info: (i, 0))), (result, ANY)],
            [
                (
                    shape((tok_count, width), B16),
                    pl.BlockSpec((quarter, width), lambda i, info: ((1 - info[0]) * 4 + i, 0)),
                )
            ],
            aliases={1: 0},
            grid=(4,),
        )[0]

    layer_out = place_partner(layer_out, out_rows, "out")

    def weight_sum(name, a, b, a_rows=0):
        order = ORDERS.get(name, tuple(masks)) if len(masks) == 3 else tuple(masks)
        columns = b[0].shape[-1]
        total = a[0].shape[1]
        half = total // 2
        grouped = len(b[0].shape) == 3
        groups = b[0].shape[0] if grouped else 1
        block = half if grouped else min(256, half)
        count = groups if grouped else half // block
        place = 2 * bit_index(order[0])

        def product(s, keep, came=None):
            step = f"{name}_{('own', 'peer')[s]}_{('s', 'k')[keep]}"
            at = place + (1 if keep else 2)
            if grouped:
                a_spec = pl.BlockSpec((rows, block), lambda i, info: (info[0] * a_rows, info[at]))
                b_spec = pl.BlockSpec((1, rows, columns), lambda i, info: (i, 0, 0))
                out_spec = pl.BlockSpec((1, half, columns), lambda i, info: (i, 0, 0))
            else:
                a_spec = pl.BlockSpec((rows, block), lambda i, info: (0, info[at] * count + i))
                b_spec = whole(b[s])
                out_spec = pl.BlockSpec((1, block, columns), lambda i, info: (0, i, 0))
            ins = [(a[s], a_spec), (b[s], b_spec)]
            if came is not None:
                ins.append((came, out_spec))
            return call(
                weight_body,
                step,
                scalar,
                ins,
                [(shape((groups, half, columns), B16), out_spec)],
                grid=(count,),
                flops=2 * rows * half * columns * groups,
            )[0]

        halves = []
        for keep in (0, 1):
            came = swap(product(1, keep), f"{name}_core_{('s', 'k')[keep]}")
            halves.append(product(0, keep, came))
        return NarrowSum(name, order, scalar).run(*halves)

    grad_down_w = weight_sum("down", active, (grad_two_low, grad_two_low))[0]
    grad_up_w = weight_sum("up", (hidden_low, hidden_low), kept_upper)[0]

    kept, grad_one, stats_one = None, [], []
    for k in range(CHUNKS):
        results = run(
            first_norm_body,
            "first_norm",
            k,
            full(*hidden_pairs[k], grad_two[k], *norms[k], gain_attn, *w_out),
            paged([page_wide, mixed_shape, mixed_shape], k),
            [shape((step, width), F32), stats_shape],
            kept,
            flops=4 * step * width * local_width,
        )
        kept = results[:3]
        grad_one.append(results[3])
        stats_one.append(results[4])
    grad_one_low, grad_mixed = kept[0], kept[1:]

    stacked = CHUNKS * heads // 2 * step
    grad_qkv, qv_bias = [None, None], [None, None]
    for side in (1, 0):
        grad_qkv[side], qv_bias[side] = call(
            functools.partial(attend_backward_body, side * heads // 2),
            f"attend_backward_{side}",
            scalar,
            [lens] + full(qkv[side], lse, mixed[side], grad_mixed[side]),
            [(o, whole(o)) for o in [shape((3, rows, local_width), B16), shape((8, local_width), F32)]],
            scratch=[
                pltpu.VMEM((rows, stacked), B16),
                pltpu.VMEM((rows, stacked), B16),
                pltpu.VMEM((stacked, local_width), B16),
                pltpu.VMEM((stacked, local_width), B16),
            ],
            flops=10 * rows * rows * local_width,
        )
    if local_width % 256 == 0:
        grad_out_w = weight_sum("out", mixed, (grad_one_low, grad_one_low))[0]
    else:
        peer = swap(mm_tn(mixed[1], grad_one_low).astype(B16), "out_core")
        own = mm_tn(mixed[0], grad_one_low) + peer.astype(F32)
        grad_out_w = plain_narrow_sum(own.astype(B16))
    grad_qkv_w = weight_sum("qkv", (tokens, tokens), grad_qkv, 1)

    part = call(
        input_body,
        "input_grad",
        scalar,
        full(*grad_qkv, *w_qkv),
        [(page_wide, whole(page_wide))],
        flops=12 * rows * width * local_width,
    )[0]
    low, came = outer_pair(part, "swap_input")
    quarter = rows // 4
    here = pl.BlockSpec((quarter, width), lambda i, info: (i, 0))
    grad_tokens, result = call(
        tokens_body,
        "tokens_grad",
        scalar,
        [
            (low, here),
            (came, here),
            (grad_one[0], pl.BlockSpec((quarter, width), lambda i, info: (jnp.minimum(i, 1), 0))),
            (grad_one[1], pl.BlockSpec((quarter, width), lambda i, info: (jnp.maximum(i - 2, 0), 0))),
        ],
        [
            (
                shape((tok_count, width), B16),
                pl.BlockSpec((quarter, width), lambda i, info: (info[0] * 4 + i, 0)),
            ),
            (page_wide, here),
        ],
        grid=(4,),
    )
    grad_tokens = place_partner(grad_tokens, result, "tokens")

    one = jnp.sum(sum(stats_one), axis=1)
    two = jnp.sum(sum(stats_two), axis=1)
    up = sum(up_bias)[0].reshape(2, local_hidden)
    qv = [bias[:2].reshape(-1) for bias in qv_bias]
    shared = jnp.concatenate([one, two], 0).reshape(-1)
    mine = jnp.concatenate([shared, up[0], qv[0]])
    sent = jnp.concatenate([shared, up[1], qv[1]])
    vectors = small_sum(mine + swap(sent, "swap_vectors"))
    six = vectors[: 6 * width].reshape(6, width)
    rest = vectors[6 * width :]
    grad_up_bias = rest[:local_hidden]
    grad_qv_bias = rest[local_hidden:].reshape(2, local_width)
    return (
        layer_out,
        grad_tokens,
        grad_qkv_w,
        grad_qv_bias,
        grad_out_w,
        six[0],
        six[1],
        six[2],
        grad_up_w,
        grad_up_bias,
        grad_down_w,
        six[3],
        six[4],
        six[5],
    )


def solution(mesh):
    placed = (
        P("narrow", None),
        P("narrow"),
        P(None, None, "wide"),
        P(None, "wide"),
        P("wide", None),
        P(),
        P(),
        P(),
        P(None, "wide"),
        P("wide"),
        P("wide", None),
        P(),
        P(),
        P(),
        P("narrow", None),
    )
    return jax.shard_map(
        local,
        mesh=mesh,
        in_specs=placed,
        out_specs=(
            P("narrow", None),
            P("narrow", None),
            P(None, None, "wide"),
            P(None, "wide"),
            P("wide", None),
            P(),
            P(),
            P(),
            P(None, "wide"),
            P("wide"),
            P("wide", None),
            P(),
            P(),
            P(),
        ),
        check_vma=False,
    )
```
